32 devices in a mesh: groups: 2 (over y), bank: 4 (over x, core), split: 4 (over z).
Axes of the slice: x: 2, y: 2, z: 4, core: 2. Of those that a mesh axis runs over, the one named last changes fastest.
Arguments:
- queries: bfloat16 [4096, 256], P(('groups', 'bank')), parts along dimension 0, may hold values from -48 to 48
- range_start: int32 [4096], P(('groups', 'bank')), parts along dimension 0, may hold values from 0 to 24574, as said below
- range_end: int32 [4096], P(('groups', 'bank')), parts along dimension 0, may hold values from 2 to 24576
- keys: bfloat16 [49152, 256], P(('groups', 'bank', 'split')), parts along dimension 0, may hold values from -4.5 to 4.5
- values: bfloat16 [49152, 256], P(('groups', 'bank', 'split')), parts along dimension 0, may hold values from -6 to 6
- floor_index: int32 [32], P(('groups', 'bank', 'split')), parts along dimension 0, may hold values from 0 to 7
- block_order: int32 [8], P('groups'), parts along dimension 0, may hold values from 0 to 3, each once
Outputs:
- retrieved: float32 [4096, 256], P(('groups', 'bank')), parts along dimension 0
- log_total: float32 [4096], P(('groups', 'bank')), parts along dimension 0
The draws below stay inside these ranges and needn't reach their ends.
There are 2 independent parts, one for each index of `groups`. The reference program is written for one: setup_inputs(seed, part) draws one part's arguments, and reference() takes and returns one part's arrays. A program takes and returns all parts, laid end to end along the dimension named above; each array names one. Nothing has to cross between parts.
Inputs may be any that keep to these rules, and one draw needn't show every extreme that they name: range_start < range_end for every query, every range holds 2 or more items; query 0 covers all 24576 items, query 2048 - 2 covers items 0 and 1 only, and query 2048 - 1 covers the last two items only.
All inputs are finite; a program needn't handle non-finite values.
Results may differ from the reference program's by a relative error of at most 0.0015.
Values may be sent and summed in bfloat16 or wider, within the bound.
No kernel may reach another device: no remote copies, remote signals or barrier semaphores. Data moves between devices by JAX's collectives and lax.ppermute only.
A program may use at most 64 MiB of HBM per device.

```python
import math
import jax
import jax.numpy as jnp
from jax import lax

E = 256
QB = 512
TILE = 128
ITEM_DEV = 1536
QUERIES = 2048
ITEMS = 24576
SHARDS = 16
N_BANK = 4


def range_pair(key):
    range_key = jax.random.fold_in(key, 11)
    center_key, levels_key, length_key, jitter_key = jax.random.split(range_key, 4)
    blocks = QUERIES // QB
    center = jnp.repeat(jax.random.randint(center_key, (blocks,), 0, ITEMS), QB)
    levels = jnp.repeat(jax.random.randint(levels_key, (blocks,), 0, 6), QB)
    extent = ITEMS // 2 ** levels
    length = 2 + jax.random.randint(length_key, (QUERIES,), 0, 2 ** 30) % jnp.maximum(extent - 1, 1)
    jitter = jax.random.randint(jitter_key, (QUERIES,), -(ITEMS // 32), ITEMS // 32 + 1)
    first = jnp.clip(center + jitter - length // 2, 0, ITEMS - length)
    last = first + length
    first = first.at[0].set(0)
    last = last.at[0].set(ITEMS)
    first = first.at[QUERIES - 2].set(0)
    last = last.at[QUERIES - 2].set(2)
    first = first.at[QUERIES - 1].set(ITEMS - 2)
    last = last.at[QUERIES - 1].set(ITEMS)
    return (first, last)


def draw_range_start(key, part):
    return range_pair(key)[0]


def draw_range_end(key, part):
    return range_pair(key)[1]


def draw_keys(key, part):
    drawn = jnp.clip(jax.random.normal(jax.random.fold_in(key, 21), (ITEMS, E), jnp.float32), -4.5, 4.5)
    return drawn.astype(jnp.bfloat16)


def draw_queries(key, part):
    drawn = jnp.clip(jax.random.normal(jax.random.fold_in(key, 31), (QUERIES, E), jnp.float32), -6.0, 6.0)
    return drawn.astype(jnp.bfloat16)


def set_ends(values, stream_key, smallest, top_value):
    spot = [jax.random.randint(jax.random.fold_in(stream_key, axis), (), 0, length) for axis, length in enumerate(values.shape)]
    longest = values.shape.index(max(values.shape))
    neighbour = spot[:longest] + [(spot[longest] + 1) % values.shape[longest]] + spot[longest + 1:]
    return values.at[tuple(spot)].set(smallest).at[tuple(neighbour)].set(top_value)


def level_of(rng, shape, shards, low, largest):
    level = 1.0
    for position, shards_of in shards:
        draws = jax.random.uniform(jax.random.fold_in(jax.random.fold_in(rng, 6), position), (shards_of,), jnp.float32, low / len(shards), largest / len(shards))
        level = level * jnp.repeat(jnp.exp(draws), shape[position] // shards_of).reshape((-1,) + (1,) * (len(shape) - 1 - position))
    return level


def centred(stream_key, shape, scale, limit, cuts=(), kind=jnp.bfloat16):
    drawn = scale * jax.random.normal(stream_key, shape, jnp.float32)
    if cuts:
        drawn = drawn * level_of(stream_key, shape, cuts, -0.22, 0.18)
    return jnp.clip(drawn, -limit, limit).astype(kind)


def setup_inputs(seed: int = 0, part: int = 0) -> dict:
    key_list = jax.random.split(jax.random.key(seed), 8)
    own_keys = jax.random.split(jax.random.fold_in(key_list[7], part), 8)
    queries = draw_queries(jax.random.fold_in(jax.random.fold_in(key_list[7], part), 71), part)
    range_start = draw_range_start(jax.random.fold_in(jax.random.fold_in(key_list[7], part), 71), part)
    range_end = draw_range_end(jax.random.fold_in(jax.random.fold_in(key_list[7], part), 71), part)
    keys = draw_keys(jax.random.fold_in(jax.random.fold_in(key_list[7], part), 71), part)
    values = centred(own_keys[4], (ITEMS, E), 1.0, 6.0, ((0, 16),))
    floor_index = set_ends(jax.random.randint(own_keys[5], (SHARDS,), 0, 8), jax.random.fold_in(own_keys[5], 1), 0, 7).astype(jnp.int32)
    block_order = jax.random.permutation(own_keys[6], N_BANK).astype(jnp.int32)
    return {"queries": queries, "range_start": range_start, "range_end": range_end, "keys": keys, "values": values, "floor_index": floor_index, "block_order": block_order}


NEG = -1e+30

def fold_items(carry, query_rows, starts, ends, key_rows, value_rows, offset, floor_value, scale):
    peak, total, pooled = carry
    scores = jnp.dot(query_rows, key_rows.T, preferred_element_type=jnp.float32) * scale
    scores = jnp.maximum(scores, floor_value)
    positions = offset + jnp.arange(key_rows.shape[0], dtype=jnp.int32)
    inside = (positions[None, :] >= starts[:, None]) & (positions[None, :] < ends[:, None])
    tile_peak = lax.optimization_barrier(jnp.max(jnp.where(inside, scores, NEG), axis=1))
    new_peak = jnp.maximum(peak, tile_peak)
    weights = jnp.where(inside, jnp.exp(scores - new_peak[:, None]), 0.0)
    factor = jnp.exp(peak - new_peak)
    total = factor * total + lax.optimization_barrier(jnp.sum(weights, axis=1))
    low_weights = weights.astype(jnp.bfloat16)
    pooled = factor[:, None] * pooled + jnp.dot(low_weights, value_rows, preferred_element_type=jnp.float32)
    return (new_peak, total, pooled)

def reference(queries, range_start, range_end, keys, values, floor_index, block_order):
    scale = 2.0 / math.sqrt(E)
    shard_count = ITEMS // ITEM_DEV
    tile_count = ITEMS // TILE
    key_tiles = keys.reshape(tile_count, TILE, E)
    value_tiles = values.reshape(tile_count, TILE, E)
    tile_offsets = jnp.arange(tile_count, dtype=jnp.int32) * TILE
    floors = floor_index.astype(jnp.float32) * 0.5 - 2.0
    tile_floors = jnp.repeat(floors, ITEM_DEV // TILE)

    def one_block(block_id):
        first_row = (block_id * QB).astype(jnp.int32)
        query_rows = lax.dynamic_slice_in_dim(queries, first_row, QB, 0)
        starts = lax.dynamic_slice_in_dim(range_start, first_row, QB, 0)
        ends = lax.dynamic_slice_in_dim(range_end, first_row, QB, 0)
        initial = (jnp.full((QB,), NEG, jnp.float32), jnp.zeros((QB,), jnp.float32), jnp.zeros((QB, E), jnp.float32))

        def visit(carry, tile):
            key_rows, value_rows, floor_value, offset = tile
            return (fold_items(carry, query_rows, starts, ends, key_rows, value_rows, offset, floor_value, scale), None)
        result, _ = lax.scan(visit, initial, (key_tiles, value_tiles, tile_floors, tile_offsets))
        peak, total, pooled = result
        return (pooled / total[:, None], peak + jnp.log(total))
    retrieved, log_total = lax.map(one_block, block_order)
    return (retrieved.reshape(QUERIES, E), log_total.reshape(QUERIES))
```

```python
import functools
import math

import jax
import jax.numpy as jnp
from jax import lax
from jax.experimental import pallas as pl
from jax.experimental.pallas import tpu as pltpu
from jax.sharding import PartitionSpec as P

NEG = -1e30
LOW = -1e29
EMPTY = -16000.0
LOG2E = math.log2(math.e)
LN2 = math.log(2.0)
FAR = 1 << 28
MIN32 = -(1 << 31)
LANES = 128
STATS = 16
TOP = 32700.0
VMEM = pl.BlockSpec(memory_space=pltpu.VMEM)
SMEM = pl.BlockSpec(memory_space=pltpu.SMEM)
ANY = pl.BlockSpec(memory_space=pl.ANY)


def pack(pooled, lse):
    width, lanes = pooled.shape
    largest = jnp.maximum(jnp.max(jnp.abs(pooled), axis=0, keepdims=True), 1e-30)
    power = jnp.ceil(128.0 * jnp.log2(largest))
    coded = jnp.floor(pooled * (TOP * jnp.exp2(power * (-1.0 / 128.0))) + 0.5)
    high = jnp.floor(lse * 2.0 + 0.5)
    low = jnp.floor((lse - high * 0.5) * 65536.0 + 0.5)
    row = lax.broadcasted_iota(jnp.int32, (STATS, lanes), 0)
    stats = jnp.where(row == 0, power, jnp.where(row == 1, high, jnp.where(row == 2, low, 0.0)))
    return coded.astype(jnp.int32).astype(jnp.int16), stats.astype(jnp.int32).astype(jnp.int16)


def unpack_stats(stats):
    stats = stats.astype(jnp.int32).astype(jnp.float32)
    scale = jnp.exp2(stats[0:1] * (1.0 / 128.0)) * (1.0 / TOP)
    return scale, stats[1:2] * 0.5 + stats[2:3] * (1.0 / 65536.0)


def as_f32(coded):
    return coded.astype(jnp.int32).astype(jnp.float32)


def joined(parts, width):
    stats = [unpack_stats(load(width, STATS)) for load in parts]
    top = functools.reduce(jnp.maximum, [lse for _, lse in stats])
    weights = [jnp.exp2(lse - top) for _, lse in stats]
    total = functools.reduce(jnp.add, weights)
    inverse = 1.0 / total
    pooled = None
    for load, (scale, _), weight in zip(parts, stats, weights):
        term = as_f32(load(0, width)) * (weight * scale * inverse)
        pooled = term if pooled is None else pooled + term
    return pack(pooled, top + jnp.log2(total))


def flash_kernel(sc, q0, q1, own_b, k0, k1, v0, v1, out, qb, fl, kb, vb, s0, s1, acc, sem, *, tile, scale):
    n, width = k0.shape
    lanes = q0.shape[0] - STATS
    count_tiles = n // tile
    groups = tile // 8
    copies = (
        (q0, qb.at[0]), (q1, qb.at[1]),
        (own_b.at[pl.ds(lanes, STATS)], fl.at[0]), (sc[1].at[pl.ds(lanes, STATS)], fl.at[1]),
        (k0, kb.at[pl.ds(0, n)]), (k1, kb.at[pl.ds(n, n)]),
        (v0, vb.at[pl.ds(0, n)]), (v1, vb.at[pl.ds(n, n)]),
    )
    sc = sc[0]
    started = [pltpu.make_async_copy(a, b, sem.at[i]) for i, (a, b) in enumerate(copies)]
    for copy in started:
        copy.start()
    for copy in started:
        copy.wait()
    sub = lax.broadcasted_iota(jnp.int32, (8, lanes), 0)
    first0, first1, flip = sc[0], sc[1], sc[2]
    floors = [fl[i].astype(jnp.float32)[6:7] * (0.5 * LOG2E) - 2.0 * LOG2E for i in range(2)]
    scores = (s0, s1)

    @pl.loop(0, 2)
    def _(half):
        query = qb[half, :lanes, :]
        code = qb[half, lanes:, :].astype(jnp.float32)
        start = (code[2:3] * 4096 + code[1:2] * 64 + code[0:1]).astype(jnp.int32)
        end = (code[5:6] * 4096 + code[4:5] * 64 + code[3:4]).astype(jnp.int32)
        lowest, highest = jnp.min(start), jnp.max(end)
        length = (end - start) + jnp.int32(MIN32)

        def bounds(first):
            a = jnp.minimum(lax.div(jnp.maximum(lowest - first, 0), tile), count_tiles)
            b = jnp.minimum(lax.div(jnp.maximum(highest - first, 0) + (tile - 1), tile), count_tiles)
            return a, jnp.maximum(b - a, 0)

        a0, c0 = bounds(first0)
        a1, c1 = bounds(first1)
        count = c0 + c1

        def place(v):
            own = v < c0
            at = jnp.clip(jnp.where(own, a0 + v, a1 + v - c0), 0, count_tiles - 1)
            offset = pl.multiple_of(jnp.where(own, 0, n) + at * tile, tile)
            return own, offset, jnp.where(v < count, jnp.where(own, first0, first1) + at * tile, FAR)

        def score(v, buf, peak):
            own, offset, base = place(v)
            s = lax.dot_general(
                kb[pl.ds(offset, tile), :], query, (((1,), (1,)), ((), ())), preferred_element_type=jnp.float32
            )
            s = jnp.maximum(s * (scale * LOG2E), jnp.where(own, floors[0], floors[1])).reshape(groups, 8, lanes)
            from_start = sub + (base - start) + jnp.int32(MIN32)
            parts = []
            for r in range(groups):
                x = jnp.where(from_start + 8 * r < length, s[r], NEG)
                buf[pl.ds(8 * r, 8), :] = x
                parts.append(x)
            while len(parts) > 1:
                parts = [jnp.maximum(a, b) for a, b in zip(parts[::2], parts[1::2])] + parts[len(parts) // 2 * 2:]
            new = jnp.maximum(peak, jnp.max(parts[0], axis=0, keepdims=True))
            return new, jnp.exp2(peak - new)

        def fold(v, buf, peak, factor, mass):
            _, offset, _ = place(v)
            weight = jnp.exp2(buf[...] - peak)
            acc[...] = acc[...] * factor + lax.dot_general(
                vb[pl.ds(offset, tile), :], weight.astype(jnp.bfloat16), (((0,), (0,)), ((), ())),
                preferred_element_type=jnp.float32,
            )
            return mass * factor + jnp.sum(weight.reshape(groups, 8, lanes), axis=0)

        acc[...] = jnp.zeros_like(acc)
        peak, factor = score(0, s0, jnp.full((1, lanes), LOW, jnp.float32))

        def body(i, carry):
            peak, factor, mass = carry
            for u in range(2):
                v = 2 * i + u
                new_peak, new_factor = score(v + 1, scores[1 - u], peak)
                mass = fold(v, scores[u], peak, factor, mass)
                peak, factor = new_peak, new_factor
            return peak, factor, mass

        peak, _, mass = lax.fori_loop(
            0, lax.div(count + 1, 2), body, (peak, factor, jnp.zeros((8, lanes), jnp.float32))
        )
        mass = jnp.sum(mass, axis=0, keepdims=True)
        safe = jnp.maximum(mass, 1.0)
        lse = jnp.where(mass > 0, peak + jnp.log2(safe), EMPTY)
        coded, stats = pack(acc[...] * (1.0 / safe), lse)
        for u in range(lanes // LANES):
            slot = jnp.bitwise_xor(2 * u + half, flip)
            out[slot, :width, :] = coded[:, u * LANES:(u + 1) * LANES]
            out[slot, width:, :] = stats[:, u * LANES:(u + 1) * LANES]


def flash(sc, q0, q1, own, partner, k0, k1, v0, v1, scale):
    n, width = k0.shape
    rows = q0.shape[0]
    lanes = rows - STATS
    tile = 512 if n % 512 == 0 else 128

    def kernel(sc_ref, q0_ref, q1_ref, own_ref, partner_ref, *refs):
        flash_kernel((sc_ref, partner_ref), q0_ref, q1_ref, own_ref, *refs, tile=tile, scale=scale)

    return pl.pallas_call(
        kernel,
        out_shape=jax.ShapeDtypeStruct((2 * lanes // LANES, width + STATS, LANES), jnp.int16),
        in_specs=[SMEM] + [ANY] * 8,
        out_specs=VMEM,
        scratch_shapes=[
            pltpu.VMEM((2, rows, width), jnp.bfloat16),
            pltpu.VMEM((2, STATS, width), jnp.bfloat16),
            pltpu.VMEM((2 * n, width), jnp.bfloat16),
            pltpu.VMEM((2 * n, width), jnp.bfloat16),
            pltpu.VMEM((tile, lanes), jnp.float32),
            pltpu.VMEM((tile, lanes), jnp.float32),
            pltpu.VMEM((width, lanes), jnp.float32),
            pltpu.SemaphoreType.DMA((8,)),
        ],
        name="flash",
    )(sc, q0, q1, own, partner, k0, k1, v0, v1)


def spread_kernel(sc, order, *refs, n_bank, width):
    *parts, out = refs
    n_groups, rows, lanes = parts[0].shape
    bank, odd = sc[0], sc[1]
    row = lax.broadcasted_iota(jnp.int32, (STATS, lanes), 0)
    nothing = jnp.where(row == 1, 2.0 * EMPTY, 0.0).astype(jnp.int32).astype(jnp.int16)
    for m in range(n_bank):
        out[m, :width, :] = jnp.zeros((width, lanes), jnp.int16)
        out[m, width:, :] = nothing
    for g in range(n_groups):
        block = jnp.bitwise_xor(bank, 2 * g + odd)
        slot = jnp.int32(0)
        for j in range(n_bank):
            slot = jnp.where(order[j] == block, jnp.bitwise_xor(bank, j), slot)
        loaders = [lambda at, size, part=part: part[g, at:at + size, :] for part in parts]
        coded, stats = joined(loaders, width)
        out[slot, :width, :] = coded
        out[slot, width:, :] = stats


def gather_kernel(*refs, width):
    *parts, out = refs
    coded, stats = joined([lambda at, size, part=part: part[at:at + size, :] for part in parts], width)
    out[:width, :] = coded
    out[width:, :] = stats


def final_kernel(sc, *refs, width):
    *parts, retrieved, log_total = refs
    lanes = parts[0].shape[1]
    for k, part in enumerate(parts):
        at = jnp.bitwise_xor(sc[0], k)
        scale, lse = unpack_stats(part[width:, :])
        retrieved[pl.ds(pl.multiple_of(at * lanes, lanes), lanes), :] = (as_f32(part[:width, :]) * scale).T
        log_total[pl.ds(at, 1), :] = lse * LN2


def local(queries, range_start, range_end, keys, values, floor_index, block_order):
    n_bank = lax.axis_size("bank")
    n_split = lax.axis_size("split")
    bank, split = lax.axis_index("bank"), lax.axis_index("split")
    n_items, width = keys.shape
    block_rows = queries.shape[0]
    lanes = block_rows // 2
    per = block_rows // n_split
    shares = LANES // per
    scale = 2.0 / math.sqrt(width)

    def over(axis, mask):
        size = lax.axis_size(axis)
        return lambda a: lax.ppermute(a, axis, [(i, i ^ mask) for i in range(size)])

    def digits(a):
        return [a & 63, (a >> 6) & 63, a >> 12]

    floor_row = jnp.broadcast_to(floor_index, (block_rows,))
    zero = jnp.zeros((block_rows,), jnp.int32)
    code = jnp.stack(digits(range_start) + digits(range_end) + [floor_row] + [zero] * (STATS - 7))
    code = code.astype(jnp.bfloat16).reshape(STATS, lanes // LANES, 2, LANES)
    tiles = queries.reshape(lanes // LANES, 2, LANES, width)
    even, odd = (
        jnp.concatenate([tiles[:, i].reshape(lanes, width), code[:, :, i].reshape(STATS, lanes)]) for i in range(2)
    )
    partner_odd = over("bank", 1)(odd)
    groups = [(even, partner_odd)]
    keys1 = over("bank", 1)(keys)
    for g in range(1, n_bank // 2):
        groups.append((over("bank", 2 * g)(even), over("bank", 2 * g + 1)(odd)))
    values1 = over("bank", 1)(values)

    first = (bank * n_split + split) * n_items
    first1 = ((bank ^ 1) * n_split + split) * n_items
    sc = jnp.stack([first, first1, split if shares == 1 else jnp.int32(0)]).astype(jnp.int32)
    results = []
    for q0, q1 in groups:
        tiles_out = flash(sc, q0, q1, even, partner_odd, keys, keys1, values, values1, scale)
        if shares > 1:
            cut = tiles_out.reshape(-1, width + STATS, shares, per).swapaxes(1, 2)
            cut = cut.reshape(n_split, width + STATS, per)
            tiles_out = jnp.stack(
                [lax.dynamic_index_in_dim(cut, split ^ k, 0, False) for k in range(n_split)]
            )
        results.append(tiles_out)
    messages = [jnp.stack([result[k] for result in results]) for k in range(n_split)]
    parts = [messages[0]] + [over("split", k)(messages[k]) for k in range(1, n_split)]
    odd_tile = (split // shares) & 1
    spread = pl.pallas_call(
        functools.partial(spread_kernel, n_bank=n_bank, width=width),
        out_shape=jax.ShapeDtypeStruct((n_bank, width + STATS, per), jnp.int16),
        in_specs=[SMEM, SMEM] + [VMEM] * n_split,
        out_specs=VMEM,
        name="spread",
    )(jnp.stack([bank, odd_tile]).astype(jnp.int32), block_order, *parts)
    parts = [spread[0]] + [over("bank", m)(spread[m]) for m in range(1, n_bank)]
    own = pl.pallas_call(
        functools.partial(gather_kernel, width=width),
        out_shape=jax.ShapeDtypeStruct((width + STATS, per), jnp.int16),
        in_specs=[VMEM] * n_bank,
        out_specs=VMEM,
        name="gather",
    )(*parts)
    parts = [own] + [over("split", k)(own) for k in range(1, n_split)]
    retrieved, log_total = pl.pallas_call(
        functools.partial(final_kernel, width=width),
        out_shape=(
            jax.ShapeDtypeStruct((block_rows, width), jnp.float32),
            jax.ShapeDtypeStruct((n_split, per), jnp.float32),
        ),
        in_specs=[SMEM] + [VMEM] * n_split,
        out_specs=(VMEM, VMEM),
        name="final",
    )(split.reshape(1).astype(jnp.int32), *parts)
    return retrieved, log_total.reshape(block_rows)


def solution(mesh):
    in_specs = (
        P(("groups", "bank"), None),
        P(("groups", "bank")),
        P(("groups", "bank")),
        P(("groups", "bank", "split"), None),
        P(("groups", "bank", "split"), None),
        P(("groups", "bank", "split")),
        P("groups"),
    )
    out_specs = (P(("groups", "bank"), None), P(("groups", "bank")))
    return jax.shard_map(local, mesh=mesh, in_specs=in_specs, out_specs=out_specs, check_vma=False)
```

```python
import functools
import math

import jax
import jax.numpy as jnp
from jax import lax
from jax.experimental import pallas as pl
from jax.experimental.pallas import tpu as pltpu
from jax.sharding import PartitionSpec as P

NEG = -1e30
LOW = -1e29
EMPTY = -16000.0
LOG2E = math.log2(math.e)
LN2 = math.log(2.0)
FAR = 1 << 28
MIN32 = -(1 << 31)
LANES = 128
STATS = 16
TOP = 32700.0
TILE_ITEMS = 1536
VMEM = pl.BlockSpec(memory_space=pltpu.VMEM)
SMEM = pl.BlockSpec(memory_space=pltpu.SMEM)
ANY = pl.BlockSpec(memory_space=pl.ANY)


def resident(a):
    return pltpu.with_memory_space_constraint(a, pltpu.VMEM)


def pack(pooled, lse):
    width, lanes = pooled.shape
    largest = jnp.maximum(jnp.max(jnp.abs(pooled), axis=0, keepdims=True), 1e-30)
    power = jnp.ceil(128.0 * jnp.log2(largest))
    coded = jnp.floor(pooled * (TOP * jnp.exp2(power * (-1.0 / 128.0))) + 0.5)
    high = jnp.floor(lse * 2.0 + 0.5)
    low = jnp.floor((lse - high * 0.5) * 65536.0 + 0.5)
    row = lax.broadcasted_iota(jnp.int32, (STATS, lanes), 0)
    stats = jnp.where(row == 0, power, jnp.where(row == 1, high, jnp.where(row == 2, low, 0.0)))
    return coded.astype(jnp.int32).astype(jnp.int16), stats.astype(jnp.int32).astype(jnp.int16)


def unpack_stats(stats):
    stats = stats.astype(jnp.int32).astype(jnp.float32)
    scale = jnp.exp2(stats[0:1] * (1.0 / 128.0)) * (1.0 / TOP)
    return scale, stats[1:2] * 0.5 + stats[2:3] * (1.0 / 65536.0)


def as_f32(coded):
    return coded.astype(jnp.int32).astype(jnp.float32)


def joined(parts, width):
    stats = [unpack_stats(load(width, STATS)) for load in parts]
    top = functools.reduce(jnp.maximum, [lse for _, lse in stats])
    weights = [jnp.exp2(lse - top) for _, lse in stats]
    total = functools.reduce(jnp.add, weights)
    inverse = 1.0 / total
    pooled = None
    for load, (scale, _), weight in zip(parts, stats, weights):
        term = as_f32(load(0, width)) * (weight * scale * inverse)
        pooled = term if pooled is None else pooled + term
    return pack(pooled, top + jnp.log2(total))


def flash_kernel(*refs, tile, chunk, scale, n_before):
    refs = list(refs)
    take = lambda count: [refs.pop(0) for _ in range(count)]
    query_ref, range_ref = take(2)
    sources = [take(3) for _ in range(2)]
    take(1)
    before = take(n_before or 0)
    score_ref, acc, *coded_refs = refs[-3:] if n_before is not None else (refs[-2], refs[-1], refs[0])
    outs = refs[:-3] if n_before is not None else []
    coded_ref = coded_refs[0]
    n, width = sources[0][1].shape
    rows = query_ref.shape[0]
    lanes = score_ref.shape[1]
    n_split = lax.axis_size("split")
    bank, split = lax.axis_index("bank"), lax.axis_index("split")
    sub = lax.broadcasted_iota(jnp.int32, (8, lanes), 0)

    @pl.loop(0, rows // lanes)
    def _(half):
        across = pl.ds(pl.multiple_of(half * lanes, lanes), lanes)
        query = query_ref[across, :]
        start, end = range_ref[0:1, across], range_ref[1:2, across]
        lowest, highest = jnp.min(start), jnp.max(end)
        length = (end - start) + jnp.int32(MIN32)
        peak = jnp.full((1, lanes), LOW, jnp.float32)
        bounds = []
        for number, (floor_ref, key_ref, _) in enumerate(sources):
            first = (jnp.bitwise_xor(bank, number) * n_split + split) * n
            floor = floor_ref[0].astype(jnp.float32) * (0.5 * LOG2E) - 2.0 * LOG2E
            begin = jnp.minimum(lax.div(jnp.maximum(lowest - first, 0), tile), n // tile)
            stop = jnp.minimum(lax.div(jnp.maximum(highest - first, 0) + (tile - 1), tile), n // tile)
            bounds.append((begin, stop))

            def score(t, peak, key_ref=key_ref, first=first, floor=floor, number=number):
                offset = pl.multiple_of(t * tile, tile)
                s = lax.dot_general(
                    key_ref[pl.ds(offset, tile), :], query, (((1,), (1,)), ((), ())),
                    preferred_element_type=jnp.float32,
                )
                s = jnp.maximum(s * (scale * LOG2E), floor).reshape(tile // 8, 8, lanes)
                from_start = sub + (first + offset - start) + jnp.int32(MIN32)
                parts = []
                for r in range(tile // 8):
                    x = jnp.where(from_start + 8 * r < length, s[r], NEG)
                    score_ref[pl.ds(number * n + offset + 8 * r, 8), :] = x
                    parts.append(x)
                while len(parts) > 1:
                    parts = [jnp.maximum(a, b) for a, b in zip(parts[::2], parts[1::2])] + parts[len(parts) // 2 * 2:]
                return jnp.maximum(peak, jnp.max(parts[0], axis=0, keepdims=True))

            peak = lax.fori_loop(begin, stop, score, peak)
        acc[...] = jnp.zeros_like(acc)
        mass = jnp.zeros((8, lanes), jnp.float32)
        for number, (_, _, value_ref) in enumerate(sources):

            def fold(t, mass, value_ref=value_ref, number=number):
                offset = pl.multiple_of(t * tile, tile)
                low = []
                for c in range(0, tile, chunk):
                    weight = jnp.exp2(score_ref[pl.ds(number * n + offset + c, chunk), :] - peak)
                    mass = mass + jnp.sum(weight.reshape(chunk // 8, 8, lanes), axis=0)
                    low.append(weight.astype(jnp.bfloat16))
                acc[...] += lax.dot_general(
                    value_ref[pl.ds(offset, tile), :], jnp.concatenate(low), (((0,), (0,)), ((), ())),
                    preferred_element_type=jnp.float32,
                )
                return mass

            mass = lax.fori_loop(*bounds[number], fold, mass)
        mass = jnp.sum(mass, axis=0, keepdims=True)
        safe = jnp.maximum(mass, 1.0)
        lse = jnp.where(mass > 0, peak + jnp.log2(safe), EMPTY)
        coded, stats = pack(acc[...] * (1.0 / safe), lse)
        for u in range(lanes // LANES):
            coded_ref[half * (lanes // LANES) + u, :width, :] = coded[:, u * LANES:(u + 1) * LANES]
            coded_ref[half * (lanes // LANES) + u, width:, :] = stats[:, u * LANES:(u + 1) * LANES]

    for k, out in enumerate(outs):
        per = out.shape[2]
        shares = LANES // per
        to = jnp.bitwise_xor(split, k)
        for g, source in enumerate([*before, coded_ref]):
            if shares == 1:
                out[g] = source[to]
                continue
            whole = source[lax.div(to, shares)].astype(jnp.int32)
            for u in range(shares):
                @pl.when(lax.rem(to, shares) == u)
                def _():
                    out[g] = whole[:, u * per:(u + 1) * per].astype(jnp.int16)


def flash(query, ranges, sources, after, before, scale, n_split):
    n, width = sources[0][1].shape
    rows = query.shape[0]
    lanes = min(256, rows)
    tile = TILE_ITEMS if n % TILE_ITEMS == 0 else 128
    coded = pltpu.VMEM((rows // LANES, width + STATS, LANES), jnp.int16)
    scratch = [pltpu.VMEM((2 * n, lanes), jnp.float32), pltpu.VMEM((width, lanes), jnp.float32)]
    out_shape = coded
    if before is not None:
        out_shape = [pltpu.VMEM((len(before) + 1, width + STATS, rows // n_split), jnp.int16)] * n_split
        scratch.append(coded)
    return pl.pallas_call(
        functools.partial(
            flash_kernel, tile=tile, chunk=min(tile, 256), scale=scale,
            n_before=None if before is None else len(before),
        ),
        out_shape=out_shape,
        in_specs=[VMEM] * 2 + [SMEM, VMEM, VMEM] * 2 + [ANY] + [VMEM] * len(before or ()),
        out_specs=VMEM if before is None else [VMEM] * n_split,
        scratch_shapes=scratch,
        compiler_params=pltpu.CompilerParams(vmem_limit_bytes=16 << 20),
        name="flash",
    )(
        resident(query), resident(ranges), *[b for f, k, v in sources for b in (f, resident(k), resident(v))], after,
        *map(resident, before or ()),
    )


def spread_kernel(order, *refs, n_bank, width):
    refs = list(refs)
    scratch = refs.pop()
    n_groups = scratch.shape[0] - 1
    parts, outs = refs[:-n_bank], refs[-n_bank:]
    bank = lax.axis_index("bank")
    lanes = scratch.shape[2]
    for g in range(n_groups):
        coded, stats = joined([lambda at, size, part=part: part[g, at:at + size, :] for part in parts], width)
        scratch[g, :width, :] = coded
        scratch[g, width:, :] = stats
    row = lax.broadcasted_iota(jnp.int32, (STATS, lanes), 0)
    scratch[n_groups, :width, :] = jnp.zeros((width, lanes), jnp.int16)
    scratch[n_groups, width:, :] = jnp.where(row == 1, 2.0 * EMPTY, 0.0).astype(jnp.int32).astype(jnp.int16)
    for m, out in enumerate(outs):
        block = order[jnp.bitwise_xor(bank, m)]
        which = jnp.int32(n_groups)
        for g in range(n_groups):
            which = jnp.where(block == jnp.bitwise_xor(bank, 2 * g), g, which)
        out[...] = scratch[which]


def gather_kernel(*refs, width):
    *parts, out = refs
    coded, stats = joined([lambda at, size, part=part: part[at:at + size, :] for part in parts], width)
    out[:width, :] = coded
    out[width:, :] = stats


def final_kernel(*refs, width):
    *parts, retrieved, log_total = refs
    lanes = parts[0].shape[1]
    for k, part in enumerate(parts):
        at = jnp.bitwise_xor(lax.axis_index("split"), k)
        scale, lse = unpack_stats(part[width:, :])
        retrieved[pl.ds(pl.multiple_of(at * lanes, lanes), lanes), :] = (as_f32(part[:width, :]) * scale).T
        log_total[pl.ds(at, 1), :] = lse * LN2


def local(queries, range_start, range_end, keys, values, floor_index, block_order):
    n_bank = lax.axis_size("bank")
    n_split = lax.axis_size("split")
    width = keys.shape[1]
    block_rows = queries.shape[0]
    per = block_rows // n_split
    scale = 2.0 / math.sqrt(width)

    def over(axis, mask):
        size = lax.axis_size(axis)
        return lambda a: lax.ppermute(a, axis, [(i, i ^ mask) for i in range(size)])

    ranges = jnp.stack([range_start, range_end])
    own = (floor_index, keys, values)
    partner = tuple(over("bank", 1)(a) for a in own)
    asked = [(over("bank", 2 * g)(queries), over("bank", 2 * g)(ranges)) for g in range(1, n_bank // 2)]
    coded = []
    for number, (q, r) in enumerate([(queries, ranges)] + asked):
        before = coded if number == len(asked) else None
        result = flash(q, r, [own, partner], asked[0][1], before, scale, n_split)
        coded.append(result)
    messages = coded[-1]
    parts = [messages[0]] + [over("split", k)(messages[k]) for k in range(1, n_split)]
    packed = pltpu.VMEM((width + STATS, per), jnp.int16)
    spread = pl.pallas_call(
        functools.partial(spread_kernel, n_bank=n_bank, width=width),
        out_shape=[packed] * n_bank,
        in_specs=[SMEM] + [VMEM] * n_split,
        out_specs=[VMEM] * n_bank,
        scratch_shapes=[pltpu.VMEM((len(coded) + 1, width + STATS, per), jnp.int16)],
        compiler_params=pltpu.CompilerParams(vmem_limit_bytes=16 << 20),
        name="spread",
    )(block_order, *map(resident, parts))
    parts = [spread[0]] + [over("bank", m)(spread[m]) for m in range(1, n_bank)]
    own = pl.pallas_call(
        functools.partial(gather_kernel, width=width),
        out_shape=packed,
        in_specs=[VMEM] * n_bank,
        out_specs=VMEM,
        compiler_params=pltpu.CompilerParams(vmem_limit_bytes=16 << 20),
        name="gather",
    )(*map(resident, parts))
    parts = [own] + [over("split", k)(own) for k in range(1, n_split)]
    retrieved, log_total = pl.pallas_call(
        functools.partial(final_kernel, width=width),
        out_shape=(
            jax.ShapeDtypeStruct((block_rows, width), jnp.float32),
            jax.ShapeDtypeStruct((n_split, per), jnp.float32),
        ),
        in_specs=[VMEM] * n_split,
        out_specs=(VMEM, VMEM),
        compiler_params=pltpu.CompilerParams(vmem_limit_bytes=16 << 20),
        name="final",
    )(*map(resident, parts))
    return retrieved, log_total.reshape(block_rows)


def solution(mesh):
    in_specs = (
        P(("groups", "bank"), None),
        P(("groups", "bank")),
        P(("groups", "bank")),
        P(("groups", "bank", "split"), None),
        P(("groups", "bank", "split"), None),
        P(("groups", "bank", "split")),
        P("groups"),
    )
    out_specs = (P(("groups", "bank"), None), P(("groups", "bank")))
    return jax.shard_map(local, mesh=mesh, in_specs=in_specs, out_specs=out_specs, check_vma=False)
```

```python
import functools
import math

import jax
import jax.numpy as jnp
from jax import lax
from jax.experimental import pallas as pl
from jax.experimental.pallas import tpu as pltpu
from jax.sharding import PartitionSpec as P

NEG = -1e30
LOW = -1e29
EMPTY = -16000.0
LOG2E = math.log2(math.e)
LN2 = math.log(2.0)
FAR = 1 << 28
MIN32 = -(1 << 31)
LANES = 128
STATS = 16
TOP = 32700.0
TILE_ITEMS = 1536
VMEM = pl.BlockSpec(memory_space=pltpu.VMEM)
SMEM = pl.BlockSpec(memory_space=pltpu.SMEM)


def resident(a):
    return pltpu.with_memory_space_constraint(a, pltpu.VMEM)


def pack(pooled, lse):
    width, lanes = pooled.shape
    largest = jnp.maximum(jnp.max(jnp.abs(pooled), axis=0, keepdims=True), 1e-30)
    power = jnp.ceil(128.0 * jnp.log2(largest))
    coded = jnp.floor(pooled * (TOP * jnp.exp2(power * (-1.0 / 128.0))) + 0.5)
    high = jnp.floor(lse * 2.0 + 0.5)
    low = jnp.floor((lse - high * 0.5) * 65536.0 + 0.5)
    row = lax.broadcasted_iota(jnp.int32, (STATS, lanes), 0)
    stats = jnp.where(row == 0, power, jnp.where(row == 1, high, jnp.where(row == 2, low, 0.0)))
    return coded.astype(jnp.int32).astype(jnp.int16), stats.astype(jnp.int32).astype(jnp.int16)


def unpack_stats(stats):
    stats = stats.astype(jnp.int32).astype(jnp.float32)
    scale = jnp.exp2(stats[0:1] * (1.0 / 128.0)) * (1.0 / TOP)
    return scale, stats[1:2] * 0.5 + stats[2:3] * (1.0 / 65536.0)


def as_f32(coded):
    return coded.astype(jnp.int32).astype(jnp.float32)


def joined(parts, width):
    stats = [unpack_stats(load(width, STATS)) for load in parts]
    top = functools.reduce(jnp.maximum, [lse for _, lse in stats])
    weights = [jnp.exp2(lse - top) for _, lse in stats]
    total = functools.reduce(jnp.add, weights)
    inverse = 1.0 / total
    pooled = None
    for load, (scale, _), weight in zip(parts, stats, weights):
        term = as_f32(load(0, width)) * (weight * scale * inverse)
        pooled = term if pooled is None else pooled + term
    return pack(pooled, top + jnp.log2(total))


def flash_kernel(*refs, tile, chunk, scale, n_before):
    refs = list(refs)
    take = lambda count: [refs.pop(0) for _ in range(count)]
    asked_ref = take(1)[0]
    sources = [take(3) for _ in range(2)]
    before = take(n_before or 0)
    score_ref, acc, *coded_refs = refs[-3:] if n_before is not None else (refs[-2], refs[-1], refs[0])
    outs = refs[:-3] if n_before is not None else []
    coded_ref = coded_refs[0]
    n, width = sources[0][1].shape
    lanes = score_ref.shape[1]
    blocks = asked_ref.shape[0] // (width + STATS)
    rows = blocks * lanes
    n_split = lax.axis_size("split")
    bank, split = lax.axis_index("bank"), lax.axis_index("split")
    sub = lax.broadcasted_iota(jnp.int32, (8, lanes), 0)

    @pl.loop(0, rows // lanes)
    def _(half):
        across = pl.ds(pl.multiple_of(half * lanes, lanes), lanes)
        query = asked_ref[across, :]
        code = asked_ref[pl.ds(pl.multiple_of(rows + half * STATS, STATS), STATS), :].astype(jnp.float32)
        start = (code[2:3] * 4096 + code[1:2] * 64 + code[0:1]).astype(jnp.int32)
        end = (code[5:6] * 4096 + code[4:5] * 64 + code[3:4]).astype(jnp.int32)
        lowest, highest = jnp.min(start), jnp.max(end)
        length = (end - start) + jnp.int32(MIN32)
        peak = jnp.full((1, lanes), LOW, jnp.float32)
        bounds = []
        for number, (floor_ref, key_ref, _) in enumerate(sources):
            first = (jnp.bitwise_xor(bank, number) * n_split + split) * n
            floor = floor_ref[0].astype(jnp.float32) * (0.5 * LOG2E) - 2.0 * LOG2E
            begin = jnp.minimum(lax.div(jnp.maximum(lowest - first, 0), tile), n // tile)
            stop = jnp.minimum(lax.div(jnp.maximum(highest - first, 0) + (tile - 1), tile), n // tile)
            bounds.append((begin, stop))

            def score(t, peak, key_ref=key_ref, first=first, floor=floor, number=number):
                offset = pl.multiple_of(t * tile, tile)
                s = lax.dot_general(
                    key_ref[pl.ds(offset, tile), :], query, (((1,), (1,)), ((), ())),
                    preferred_element_type=jnp.float32,
                )
                s = jnp.maximum(s * (scale * LOG2E), floor).reshape(tile // 8, 8, lanes)
                from_start = sub + (first + offset - start) + jnp.int32(MIN32)
                parts = []
                for r in range(tile // 8):
                    x = jnp.where(from_start + 8 * r < length, s[r], NEG)
                    score_ref[pl.ds(number * n + offset + 8 * r, 8), :] = x
                    parts.append(x)
                while len(parts) > 1:
                    parts = [jnp.maximum(a, b) for a, b in zip(parts[::2], parts[1::2])] + parts[len(parts) // 2 * 2:]
                return jnp.maximum(peak, jnp.max(parts[0], axis=0, keepdims=True))

            peak = lax.fori_loop(begin, stop, score, peak)
        acc[...] = jnp.zeros_like(acc)
        mass = jnp.zeros((8, lanes), jnp.float32)
        for number, (_, _, value_ref) in enumerate(sources):

            def fold(t, mass, value_ref=value_ref, number=number):
                offset = pl.multiple_of(t * tile, tile)
                low = []
                for c in range(0, tile, chunk):
                    weight = jnp.exp2(score_ref[pl.ds(number * n + offset + c, chunk), :] - peak)
                    mass = mass + jnp.sum(weight.reshape(chunk // 8, 8, lanes), axis=0)
                    low.append(weight.astype(jnp.bfloat16))
                acc[...] += lax.dot_general(
                    value_ref[pl.ds(offset, tile), :], jnp.concatenate(low), (((0,), (0,)), ((), ())),
                    preferred_element_type=jnp.float32,
                )
                return mass

            mass = lax.fori_loop(*bounds[number], fold, mass)
        mass = jnp.sum(mass, axis=0, keepdims=True)
        safe = jnp.maximum(mass, 1.0)
        lse = jnp.where(mass > 0, peak + jnp.log2(safe), EMPTY)
        coded, stats = pack(acc[...] * (1.0 / safe), lse)
        for u in range(lanes // LANES):
            coded_ref[half * (lanes // LANES) + u, :width, :] = coded[:, u * LANES:(u + 1) * LANES]
            coded_ref[half * (lanes // LANES) + u, width:, :] = stats[:, u * LANES:(u + 1) * LANES]

    for k, out in enumerate(outs):
        per = out.shape[2]
        shares = LANES // per
        to = jnp.bitwise_xor(split, k)
        for g, source in enumerate([*before, coded_ref]):
            if shares == 1:
                out[g] = source[to]
                continue
            whole = source[lax.div(to, shares)].astype(jnp.int32)
            for u in range(shares):
                @pl.when(lax.rem(to, shares) == u)
                def _():
                    out[g] = whole[:, u * per:(u + 1) * per].astype(jnp.int16)


def flash(asked, sources, before, scale, n_split):
    n, width = sources[0][1].shape
    lanes = width
    rows = asked.shape[0] // (width + STATS) * lanes
    tile = TILE_ITEMS if n % TILE_ITEMS == 0 else 128
    coded = pltpu.VMEM((rows // LANES, width + STATS, LANES), jnp.int16)
    scratch = [pltpu.VMEM((2 * n, lanes), jnp.float32), pltpu.VMEM((width, lanes), jnp.float32)]
    out_shape = coded
    if before is not None:
        out_shape = [pltpu.VMEM((len(before) + 1, width + STATS, rows // n_split), jnp.int16)] * n_split
        scratch.append(coded)
    return pl.pallas_call(
        functools.partial(
            flash_kernel, tile=tile, chunk=min(tile, 256), scale=scale,
            n_before=None if before is None else len(before),
        ),
        out_shape=out_shape,
        in_specs=[VMEM] + [SMEM, VMEM, VMEM] * 2 + [VMEM] * len(before or ()),
        out_specs=VMEM if before is None else [VMEM] * n_split,
        scratch_shapes=scratch,
        compiler_params=pltpu.CompilerParams(vmem_limit_bytes=16 << 20),
        name="flash",
    )(
        resident(asked), *[b for f, k, v in sources for b in (f, resident(k), resident(v))],
        *map(resident, before or ()),
    )


def load_kernel(query, start, end, key, value, asked, key_out, value_out, start_ref, end_ref, sem):
    rows, width = query.shape
    pairs = (
        (start, start_ref), (end, end_ref), (query, asked.at[pl.ds(0, rows)]), (key, key_out), (value, value_out)
    )
    copies = [pltpu.make_async_copy(a, b, sem.at[i]) for i, (a, b) in enumerate(pairs)]
    for copy in copies:
        copy.start()
    for copy in copies[:2]:
        copy.wait()
    row = lax.broadcasted_iota(jnp.int32, (STATS, width), 0)
    for half in range(rows // width):
        across = pl.ds(half * width, width)
        code = jnp.zeros((STATS, width), jnp.int32)
        for at, ref in ((0, start_ref), (3, end_ref)):
            bound = ref[:, across]
            for digit in range(3):
                code = jnp.where(row == at + digit, (bound >> (6 * digit)) & 63, code)
        asked[pl.ds(rows + half * STATS, STATS), :] = code.astype(jnp.float32).astype(jnp.bfloat16)
    for copy in copies[2:]:
        copy.wait()


def loaded(query, start, end, key, value):
    rows, width = query.shape
    arrays = (query, start.reshape(1, rows), end.reshape(1, rows), key, value)
    return pl.pallas_call(
        load_kernel,
        out_shape=[
            pltpu.VMEM((rows + rows // width * STATS, width), query.dtype),
            pltpu.VMEM(key.shape, key.dtype), pltpu.VMEM(value.shape, value.dtype),
        ],
        in_specs=[pl.BlockSpec(memory_space=pltpu.HBM)] * 5,
        out_specs=[VMEM] * 3,
        scratch_shapes=[pltpu.VMEM((1, rows), jnp.int32)] * 2 + [pltpu.SemaphoreType.DMA((5,))],
        compiler_params=pltpu.CompilerParams(vmem_limit_bytes=16 << 20),
        name="load",
    )(*[pltpu.with_memory_space_constraint(a, pltpu.HBM) for a in arrays])


def spread_kernel(order, *refs, n_bank, width):
    refs = list(refs)
    scratch = refs.pop()
    n_groups = scratch.shape[0] - 1
    parts, outs = refs[:-n_bank], refs[-n_bank:]
    bank = lax.axis_index("bank")
    lanes = scratch.shape[2]
    for g in range(n_groups):
        coded, stats = joined([lambda at, size, part=part: part[g, at:at + size, :] for part in parts], width)
        scratch[g, :width, :] = coded
        scratch[g, width:, :] = stats
    row = lax.broadcasted_iota(jnp.int32, (STATS, lanes), 0)
    scratch[n_groups, :width, :] = jnp.zeros((width, lanes), jnp.int16)
    scratch[n_groups, width:, :] = jnp.where(row == 1, 2.0 * EMPTY, 0.0).astype(jnp.int32).astype(jnp.int16)
    for m, out in enumerate(outs):
        block = order[jnp.bitwise_xor(bank, m)]
        which = jnp.int32(n_groups)
        for g in range(n_groups):
            which = jnp.where(block == jnp.bitwise_xor(bank, 2 * g), g, which)
        out[...] = scratch[which]


def gather_kernel(*refs, width):
    *parts, out = refs
    coded, stats = joined([lambda at, size, part=part: part[at:at + size, :] for part in parts], width)
    out[:width, :] = coded
    out[width:, :] = stats


def final_kernel(*refs, width):
    *parts, retrieved, log_total = refs
    lanes = parts[0].shape[1]
    for k, part in enumerate(parts):
        at = jnp.bitwise_xor(lax.axis_index("split"), k)
        scale, lse = unpack_stats(part[width:, :])
        retrieved[pl.ds(pl.multiple_of(at * lanes, lanes), lanes), :] = (as_f32(part[:width, :]) * scale).T
        log_total[pl.ds(at, 1), :] = lse * LN2


def local(queries, range_start, range_end, keys, values, floor_index, block_order):
    n_bank = lax.axis_size("bank")
    n_split = lax.axis_size("split")
    width = keys.shape[1]
    block_rows = queries.shape[0]
    per = block_rows // n_split
    scale = 2.0 / math.sqrt(width)

    def over(axis, mask):
        size = lax.axis_size(axis)
        return lambda a: lax.ppermute(a, axis, [(i, i ^ mask) for i in range(size)])

    partner = tuple(over("bank", 1)(a) for a in (floor_index, keys, values))
    mine, own_keys, own_values = loaded(queries, range_start, range_end, keys, values)
    asked = [mine] + [over("bank", 2 * g)(mine) for g in range(1, n_bank // 2)]
    sources = [(floor_index, own_keys, own_values), partner]
    coded = []
    for number, block in enumerate(asked):
        before = coded if number == len(asked) - 1 else None
        coded.append(flash(block, sources, before, scale, n_split))
    messages = coded[-1]
    parts = [messages[0]] + [over("split", k)(messages[k]) for k in range(1, n_split)]
    packed = pltpu.VMEM((width + STATS, per), jnp.int16)
    spread = pl.pallas_call(
        functools.partial(spread_kernel, n_bank=n_bank, width=width),
        out_shape=[packed] * n_bank,
        in_specs=[SMEM] + [VMEM] * n_split,
        out_specs=[VMEM] * n_bank,
        scratch_shapes=[pltpu.VMEM((len(coded) + 1, width + STATS, per), jnp.int16)],
        compiler_params=pltpu.CompilerParams(vmem_limit_bytes=16 << 20),
        name="spread",
    )(block_order, *map(resident, parts))
    parts = [spread[0]] + [over("bank", m)(spread[m]) for m in range(1, n_bank)]
    own = pl.pallas_call(
        functools.partial(gather_kernel, width=width),
        out_shape=packed,
        in_specs=[VMEM] * n_bank,
        out_specs=VMEM,
        compiler_params=pltpu.CompilerParams(vmem_limit_bytes=16 << 20),
        name="gather",
    )(*map(resident, parts))
    parts = [own] + [over("split", k)(own) for k in range(1, n_split)]
    retrieved, log_total = pl.pallas_call(
        functools.partial(final_kernel, width=width),
        out_shape=(
            jax.ShapeDtypeStruct((block_rows, width), jnp.float32),
            jax.ShapeDtypeStruct((n_split, per), jnp.float32),
        ),
        in_specs=[VMEM] * n_split,
        out_specs=(VMEM, VMEM),
        compiler_params=pltpu.CompilerParams(vmem_limit_bytes=16 << 20),
        name="final",
    )(*map(resident, parts))
    return retrieved, log_total.reshape(block_rows)


def solution(mesh):
    in_specs = (
        P(("groups", "bank"), None),
        P(("groups", "bank")),
        P(("groups", "bank")),
        P(("groups", "bank", "split"), None),
        P(("groups", "bank", "split"), None),
        P(("groups", "bank", "split")),
        P("groups"),
    )
    out_specs = (P(("groups", "bank"), None), P(("groups", "bank")))
    return jax.shard_map(local, mesh=mesh, in_specs=in_specs, out_specs=out_specs, check_vma=False)
```
